32 devices in a mesh: groups: 2 (over x), tile: 16 (over z, y, core).
Axes of the slice: x: 2, y: 2, z: 4, core: 2. Of those that a mesh axis runs over, the one named last changes fastest.
Arguments:
- video_latent: bfloat16 [96, 160, 384], P(('groups', 'tile')), parts along dimension 0, may hold values from -6 to 6
- conv_cache: bfloat16 [96, 160, 384], P(('groups', 'tile')), parts along dimension 0, may hold values from -6 to 6
- norm_gain: float32 [384], replicated, may hold values from 0.1 to 1.9
- conv_kernel: bfloat16 [3, 3, 3, 384, 384], replicated, may hold values from -0.0625 to 0.0625
- attend_gain: float32 [384], replicated, may hold values from 0.1 to 1.9
- w_query: bfloat16 [384, 384], replicated, may hold values from -2 to 6
- w_key: bfloat16 [384, 384], replicated, may hold values from -2 to 6
- w_value: bfloat16 [384, 384], replicated, may hold values from -0.3125 to 0.3125
- w_output: bfloat16 [384, 384], replicated, may hold values from -0.3125 to 0.3125
Outputs:
- result: bfloat16 [96, 160, 384], P(('groups', 'tile')), parts along dimension 0
The draws below stay inside these ranges and needn't reach their ends.
There are 2 independent parts, one for each index of `groups`. The reference program is written for one: setup_inputs(seed, part) draws one part's arguments, and reference() takes and returns one part's arrays. A program takes and returns all parts, laid end to end along the dimension named above; an argument that names none is the same for every part. Nothing has to cross between parts.
All inputs are finite; a program needn't handle non-finite values.
Results may differ from the reference program's by a relative error of at most 0.007.
Values may be sent and summed in bfloat16 or wider, within the bound.
No kernel may reach another device: no remote copies, remote signals or barrier semaphores. Data moves between devices by JAX's collectives and lax.ppermute only.
A program may use at most 64 MiB of HBM per device.

```python
import jax
import jax.numpy as jnp
from jax import lax

C = 384
ROWS_DEV = 3
COLS = 160
CACHED = 2
ROW_TILES = 8
FRAMES = 2
ROWS = 24


def projection_draw(key, salt):
    matrix = jax.random.truncated_normal(jax.random.fold_in(key, salt), -4.0, 4.0, (C, C), jnp.float32) * (1.7 * float(C) ** (-0.5))
    return matrix.astype(jnp.bfloat16)


def draw_w_query(key, part):
    return projection_draw(key, 11)


def draw_w_key(key, part):
    return projection_draw(key, 12)


def level_of(rng, dims, shards, low, largest):
    level, own = 1.0, jax.random.fold_in(rng, 6)
    for position, shards_of in shards:
        draws = jnp.exp(jax.random.uniform(jax.random.fold_in(own, position), (shards_of,), jnp.float32, low / len(shards), largest / len(shards)))
        level = level * jnp.repeat(draws, dims[position] // shards_of).reshape([-1 if axis == position else 1 for axis in range(len(dims))])
    return level


def scatter_about(rng, shape, width, limit, shards=(), held_as=jnp.bfloat16):
    drawn = jax.random.normal(rng, shape, jnp.float32) * width
    if len(shards) > 0:
        drawn = level_of(rng, shape, shards, -0.22, 0.18) * drawn
    return jnp.clip(drawn, min=-limit, max=limit).astype(held_as)


def setup_inputs(seed: int = 0, part: int = 0) -> dict:
    key_list = jax.random.split(jax.random.key(seed), 10)
    own_keys = jax.random.split(jax.random.fold_in(key_list[9], part), 10)
    video_latent = scatter_about(own_keys[0], (FRAMES * ROWS, COLS, C), 1.0, 6.0, ((0, 16),))
    conv_cache = scatter_about(own_keys[1], (FRAMES * ROWS, COLS, C), 1.0, 6.0, ((0, 16),))
    norm_gain = jnp.clip(1.0 + 0.18 * jax.random.normal(key_list[2], (C,), jnp.float32), 0.1, 1.9)
    conv_kernel = scatter_about(key_list[3], (3, 3, 3, C, C), (27 * C) ** -0.5, 0.0625)
    attend_gain = jnp.clip(1.0 + 0.18 * jax.random.normal(key_list[4], (C,), jnp.float32), 0.1, 1.9)
    w_query = draw_w_query(jax.random.fold_in(key_list[9], 71), part)
    w_key = draw_w_key(jax.random.fold_in(key_list[9], 71), part)
    w_value = scatter_about(key_list[7], (C, C), C ** -0.5, 0.3125)
    w_output = scatter_about(key_list[8], (C, C), C ** -0.5, 0.3125)
    return {"video_latent": video_latent, "conv_cache": conv_cache, "norm_gain": norm_gain, "conv_kernel": conv_kernel, "attend_gain": attend_gain, "w_query": w_query, "w_key": w_key, "w_value": w_value, "w_output": w_output}


def rms_scale(inputs, scale_gain):
    floats = inputs.astype(jnp.float32)
    return floats * lax.rsqrt(lax.optimization_barrier(jnp.mean(floats * floats, axis=-1, keepdims=True)) + 1e-06) * scale_gain

def causal_conv(inputs, kernel):
    depth_in, rows_all, cols_all, channels = inputs.shape
    frames_out = depth_in - 2
    padded = jnp.pad(inputs, ((0, 0), (1, 1), (1, 1), (0, 0)))
    summed = jnp.zeros((frames_out * rows_all * cols_all, channels), jnp.float32)
    for time_tap in range(3):
        for row_tap in range(3):
            for col_tap in range(3):
                window = padded[time_tap:time_tap + frames_out, row_tap:row_tap + rows_all, col_tap:col_tap + cols_all]
                summed = summed + jnp.dot(window.reshape(-1, channels), kernel[time_tap, row_tap, col_tap], preferred_element_type=jnp.float32)
    return summed.reshape(frames_out, rows_all, cols_all, channels)

def to_frames(blocks):
    return blocks.reshape(ROW_TILES, FRAMES, ROWS_DEV, COLS, C).transpose(1, 0, 2, 3, 4).reshape(FRAMES, ROWS, COLS, C)

def reference(video_latent, conv_cache, norm_gain, conv_kernel, attend_gain, w_query, w_key, w_value, w_output):
    latent = to_frames(video_latent)
    moved_cache = jnp.roll(conv_cache.reshape(ROW_TILES, FRAMES * ROWS_DEV, COLS, C), 1, axis=0)
    earlier = to_frames(moved_cache)[FRAMES - CACHED:]
    activated = jax.nn.silu(rms_scale(latent, norm_gain)).astype(jnp.bfloat16)
    stacked = jnp.concatenate([earlier, activated], axis=0)
    residual = (latent.astype(jnp.float32) + causal_conv(stacked, conv_kernel)).astype(jnp.bfloat16)
    normed = rms_scale(residual, attend_gain).astype(jnp.bfloat16)
    flat_rows = normed.reshape(-1, C)

    def project(weight):
        return jnp.dot(flat_rows, weight, preferred_element_type=jnp.float32).astype(jnp.bfloat16).reshape(FRAMES, ROWS, COLS, C)
    queries = project(w_query)
    keys_all = project(w_key)
    values_all = project(w_value)
    score_scale = float(C) ** (-0.5)

    def one_frame(frame_data):
        frame_queries, frame_keys, frame_values = frame_data
        frame_keys = frame_keys.reshape(-1, C)
        frame_values = frame_values.reshape(-1, C)

        def one_row(row_queries):
            scores = jnp.dot(row_queries, frame_keys.T, preferred_element_type=jnp.float32) * score_scale
            highest = lax.optimization_barrier(jnp.max(scores, axis=-1, keepdims=True))
            weights = jnp.exp(scores - highest)
            weight_sum = lax.optimization_barrier(jnp.sum(weights, axis=-1, keepdims=True))
            numerator = jnp.dot(weights.astype(jnp.bfloat16), frame_values, preferred_element_type=jnp.float32)
            return (numerator / weight_sum).astype(jnp.bfloat16)
        return lax.map(one_row, frame_queries)
    attended = lax.map(one_frame, (queries, keys_all, values_all))
    output_term = jnp.dot(attended.reshape(-1, C), w_output, preferred_element_type=jnp.float32).reshape(FRAMES, ROWS, COLS, C)
    final = (residual.astype(jnp.float32) + output_term).astype(jnp.bfloat16)
    final = final.reshape(FRAMES, ROW_TILES, ROWS_DEV, COLS, C).transpose(1, 0, 2, 3, 4)
    return final.reshape(FRAMES * ROWS, COLS, C)
```

```python
import functools

import jax
import jax.numpy as jnp
from jax import lax
from jax.experimental import pallas as pl
from jax.experimental.pallas import tpu as pltpu
from jax.sharding import PartitionSpec as P

LOG2E = 1.4426950408889634
F32 = jnp.float32
BF16 = jnp.bfloat16


def params(mib, **kw):
    return pltpu.CompilerParams(vmem_limit_bytes=mib * 2**20, **kw)


def rms(values, gain):
    floats = values.astype(F32)
    return floats * lax.rsqrt(jnp.mean(floats * floats, axis=-1, keepdims=True) + 1e-06) * gain


def silu(values):
    return values / (1.0 + jnp.exp(-values))


def tap_product(rows, cols, lhs_ref, w_ref):
    span = rows * cols
    lhs = jnp.concatenate([lhs_ref[pl.ds(i * cols, span), :] for i in range(3)], axis=1)
    rhs = jnp.concatenate([w_ref[i] for i in range(3)], axis=0)
    return jnp.dot(lhs, rhs, preferred_element_type=F32)


def add_tap(rows, cols, total, product):
    span = rows * cols
    column = lax.broadcasted_iota(jnp.int32, product.shape, 0) % cols
    tap = pl.program_id(0)

    @pl.when(tap == 0)
    def _():
        total[...] += jnp.where(column == 0, 0.0, pltpu.roll(product, 1, 0))

    @pl.when(tap == 1)
    def _():
        total[...] += product

    @pl.when(tap == 2)
    def _():
        total[...] += jnp.where(column == cols - 1, 0.0, pltpu.roll(product, span - 1, 0))


def own_kernel(rows, cols, x_ref, above_ref, below_ref, gain_ref, w_ref, act_ref, total_ref):
    @pl.when(pl.program_id(0) == 0)
    def _():
        gain = gain_ref[...]
        act_ref[pl.ds(0, cols), :] = silu(rms(above_ref[...], gain)).astype(BF16)
        act_ref[pl.ds(cols, rows * cols), :] = silu(rms(x_ref[...], gain)).astype(BF16)
        act_ref[pl.ds((rows + 1) * cols, cols), :] = silu(rms(below_ref[...], gain)).astype(BF16)
        total_ref[...] = jnp.zeros_like(total_ref)

    add_tap(rows, cols, total_ref, tap_product(rows, cols, act_ref, w_ref))


def middle_kernel(rows, cols, in_ref, w_ref, before_ref, total_ref):
    @pl.when(pl.program_id(0) == 0)
    def _():
        total_ref[...] = before_ref[...]

    add_tap(rows, cols, total_ref, tap_product(rows, cols, in_ref, w_ref))


def last_kernel(rows, cols, in_ref, w_ref, before_ref, x_ref, gain_ref, res_ref, normed_ref, total):
    @pl.when(pl.program_id(0) == 0)
    def _():
        total[...] = before_ref[...] + x_ref[...].astype(F32)

    add_tap(rows, cols, total, tap_product(rows, cols, in_ref, w_ref))

    @pl.when(pl.program_id(0) == 2)
    def _():
        residual = total[...].astype(BF16)
        res_ref[...] = residual
        normed_ref[...] = rms(residual, gain_ref[...]).astype(BF16)


def whole(shape):
    return pl.BlockSpec(shape, lambda *_: (0,) * len(shape))


def weight_spec(time_tap, channels):
    return pl.BlockSpec(
        (None, 3, None, channels, channels), lambda tap: (time_tap, 0, tap, 0, 0)
    )


def score_part(query, key):
    return lax.dot_general(
        query, key, (((1,), (1,)), ((), ())), preferred_element_type=F32
    )


def first_kernel(scale, normed_ref, wq_ref, wk_ref, query_ref, high_ref, sum_ref, acc_ref):
    keys = normed_ref[...]
    query = jnp.dot(keys, wq_ref[...], preferred_element_type=F32).astype(BF16)
    query = (score_part(query, wk_ref[...]) * scale).astype(BF16)
    query_ref[...] = query
    scores = score_part(query, keys)
    high = jnp.max(scores, axis=-1, keepdims=True)
    weights = jnp.exp2(scores - high)
    high_ref[...] = jnp.broadcast_to(high, high_ref.shape)
    sum_ref[...] = jnp.broadcast_to(jnp.sum(weights, axis=-1, keepdims=True), sum_ref.shape)
    acc_ref[...] = jnp.dot(weights.astype(BF16), keys, preferred_element_type=F32)


def absorb(query, blocks, high_before, sum_before, acc_before):
    scores = [score_part(query, keys) for keys in blocks]
    high = high_before
    for part in scores:
        high = jnp.maximum(high, jnp.max(part, axis=-1, keepdims=True))
    rescale = jnp.exp2(high_before - high)
    total = sum_before * rescale
    acc = acc_before * rescale
    for part, keys in zip(scores, blocks):
        weights = jnp.exp2(part - high)
        total = total + jnp.sum(weights, axis=-1, keepdims=True)
        acc = acc + jnp.dot(weights.astype(BF16), keys, preferred_element_type=F32)
    return high, total, acc


def more_kernel(count, query_ref, *refs):
    blocks, (high_ref, sum_ref, acc_ref), (high_out, sum_out, acc_out) = (
        refs[:count], refs[count : count + 3], refs[count + 3 :]
    )
    high, total, acc = absorb(
        query_ref[...], [ref[...] for ref in blocks], high_ref[:, :1], sum_ref[:, :1], acc_ref[...]
    )
    high_out[...] = jnp.broadcast_to(high, high_out.shape)
    sum_out[...] = jnp.broadcast_to(total, sum_out.shape)
    acc_out[...] = acc


def final_kernel(count, query_ref, *refs):
    blocks, (high_ref, sum_ref, acc_ref, res_ref, wv_ref, wo_ref, out_ref) = (
        refs[:count], refs[count:]
    )
    _, total, acc = absorb(
        query_ref[...], [ref[...] for ref in blocks], high_ref[:, :1], sum_ref[:, :1], acc_ref[...]
    )
    mixed = (acc / total).astype(BF16)
    attended = jnp.dot(mixed, wv_ref[...], preferred_element_type=F32).astype(BF16)
    term = jnp.dot(attended, wo_ref[...], preferred_element_type=F32)
    out_ref[...] = (res_ref[...].astype(F32) + term).astype(BF16)


def ring_order(row_tiles):
    half = row_tiles // 2
    return [2 * k for k in range(half)] + [2 * (half - 1 - k) + 1 for k in range(half)]


def body(
    video_latent, conv_cache, norm_gain, conv_kernel, attend_gain, w_query, w_key, w_value, w_output
):
    rows, cols, channels = video_latent.shape
    span = rows * cols
    tiles = lax.axis_size("tile")
    row_tiles = min(16, tiles // 2)
    frames = tiles // row_tiles
    position = lax.axis_index("tile")
    frame = position % frames
    tile = position // frames

    def send(value, moves):
        pairs = [(a * frames + s, b * frames + t) for (a, s), (b, t) in moves]
        return lax.ppermute(value, "tile", pairs)

    flat = video_latent.reshape(span, channels)
    cache = conv_cache.reshape(span, channels)
    all_tiles = range(row_tiles)
    cached = [(frames - 2 + t, t) for t in range(2)]

    cache_block = send(
        cache, [(((r - 1) % row_tiles, s), (r, t)) for r in all_tiles for s, t in cached]
    )
    cache_above = send(
        cache[span - cols :],
        [(((r - 2) % row_tiles, s), (r, t)) for r in all_tiles[1:] for s, t in cached],
    )
    above = send(
        flat[span - cols :],
        [((r - 1, t), (r, t)) for r in all_tiles[1:] for t in range(frames)],
    )
    below = send(
        flat[:cols], [((r + 1, t), (r, t)) for r in all_tiles[:-1] for t in range(frames)]
    )
    if frames == 2:
        cache_below = jnp.where(tile < row_tiles - 1, cache[:cols], 0).astype(BF16)
    else:
        cache_below = send(
            cache[:cols], [((r, s), (r, t)) for r in all_tiles[:-1] for s, t in cached]
        )

    gain = norm_gain.reshape(1, channels)
    wide = jax.ShapeDtypeStruct((span, channels), F32)
    narrow = jax.ShapeDtypeStruct((span, channels), BF16)
    padded = jax.ShapeDtypeStruct((span + 2 * cols, channels), BF16)
    full, rim, tall, row = (span, channels), (cols, channels), padded.shape, (1, channels)
    conv_flops = 2 * span * 9 * channels * channels
    conv_cost = pl.CostEstimate(
        flops=conv_flops, bytes_accessed=18 * channels * channels, transcendentals=0
    )

    act, total = pl.pallas_call(
        functools.partial(own_kernel, rows, cols),
        grid=(3,),
        out_shape=(padded, wide),
        in_specs=[whole(full), whole(rim), whole(rim), whole(row), weight_spec(2, channels)],
        out_specs=(whole(tall), whole(full)),
        compiler_params=params(24),
        cost_estimate=conv_cost,
        name="conv_own",
    )(flat, above, below, gain, conv_kernel)

    cache_all = jnp.concatenate([cache_above, cache_block, cache_below], axis=0)
    if frames == 2:
        swap = jnp.where(frame == 0, act, cache_all)
        two_back = cache_all
        one_back = send(swap, [((r, t), (r, 1 - t)) for r in all_tiles for t in range(2)])
    else:
        later = send(
            act, [((r, t), (r, t + 1)) for r in all_tiles for t in range(frames - 1)]
        )
        first = send(cache_all, [((r, 1), (r, 0)) for r in all_tiles])
        one_back = jnp.where(frame == 0, first, later)
        earlier = send(
            act, [((r, t), (r, t + 2)) for r in all_tiles for t in range(frames - 2)]
        )
        two_back = jnp.where(frame < 2, cache_all, earlier)

    total = pl.pallas_call(
        functools.partial(middle_kernel, rows, cols),
        grid=(3,),
        out_shape=wide,
        in_specs=[whole(tall), weight_spec(0, channels), whole(full)],
        out_specs=whole(full),
        compiler_params=params(24),
        cost_estimate=conv_cost,
        name="conv_two_back",
    )(two_back, conv_kernel, total)

    residual, normed = pl.pallas_call(
        functools.partial(last_kernel, rows, cols),
        grid=(3,),
        out_shape=(narrow, narrow),
        in_specs=[
            whole(tall), weight_spec(1, channels), whole(full), whole(full), whole(row),
        ],
        out_specs=(whole(full), whole(full)),
        scratch_shapes=[pltpu.VMEM(full, F32)],
        compiler_params=params(24),
        cost_estimate=conv_cost,
        name="conv_one_back",
    )(one_back, conv_kernel, total, flat, attend_gain.reshape(1, channels))

    order = ring_order(row_tiles)
    forward = [
        ((order[k], t), (order[(k + 1) % row_tiles], t)) for k in all_tiles for t in range(frames)
    ]
    backward = [(b, a) for a, b in forward]
    arrived, right, left = [], normed, normed
    for _ in range(row_tiles // 2 - 1):
        right, left = send(right, forward), send(left, backward)
        arrived.append((right, left))
    cut = span // 2
    arrived.append((send(right[:cut], forward), send(left[cut:], backward)))

    stat = jax.ShapeDtypeStruct((span, 128), F32)
    scale = LOG2E * float(channels) ** (-0.5)
    attend_cost = lambda keys: pl.CostEstimate(
        flops=4 * span * keys * channels, bytes_accessed=2 * keys * channels,
        transcendentals=span * keys,
    )
    query, high, weight_sum, acc = pl.pallas_call(
        functools.partial(first_kernel, scale),
        out_shape=(narrow, stat, stat, wide),
        compiler_params=params(24),
        cost_estimate=attend_cost(span),
        name="attend_own",
    )(normed, w_query, w_key)
    for blocks in arrived[:-1]:
        high, weight_sum, acc = pl.pallas_call(
            functools.partial(more_kernel, len(blocks)),
            out_shape=(stat, stat, wide),
            compiler_params=params(24),
            cost_estimate=attend_cost(2 * span),
            name="attend_more",
        )(query, *blocks, high, weight_sum, acc)
    blocks = arrived[-1]
    result = pl.pallas_call(
        functools.partial(final_kernel, len(blocks)),
        out_shape=narrow,
        compiler_params=params(24),
        cost_estimate=attend_cost(span),
        name="attend_last",
    )(query, *blocks, high, weight_sum, acc, residual, w_value, w_output)
    return result.reshape(video_latent.shape)


def solution(mesh):
    spread = P(("groups", "tile"), None, None)
    return jax.shard_map(
        body,
        mesh=mesh,
        in_specs=(spread, spread) + (P(),) * 7,
        out_specs=spread,
        check_vma=False,
    )
```
